256 devices in a mesh: occ: 64 (over y, z, x_lo), virt: 4 (over x_hi, core).
Axes of the slice: x: 4 (x_hi: 2, x_lo: 2; x = x_hi * 2 + x_lo), y: 4, z: 8, core: 2. Of those that a mesh axis runs over, the one named last changes fastest.
Arguments:
- integrals: bfloat16 [64, 1024, 1536], P('occ', 'virt'), may hold values from -2 to 2
- occupied_energy: float32 [64], replicated, may hold values from -2 to -0.2
- virtual_energy: float32 [1024], replicated, may hold values from 0.5 to 4
- partner_list: int32 [2, 64], replicated, may hold values from 0 to 63, each once within a row
- tile_lists: int32 [2, 64, 4, 56], P(None, 'occ', 'virt'), may hold values from -1 to 63, as said below
Outputs:
- gradient: float32 [64, 1024, 1536], P('occ', 'virt')
The draws below stay inside these ranges and needn't reach their ends.
Inputs may be any that keep to these rules, and one draw needn't show every extreme that they name: Each row partner_list[k] holds every block number once. In each list tile_lists[k, d, s] the live entries stand first, are distinct, and number from 24 to 56; the rest are -1. For each k and d one slice s holds exactly 56 live entries.
All inputs are finite; a program needn't handle non-finite values.
Results may differ from the reference program's by a relative error of at most 0.0021.
Values may be sent and summed in bfloat16 or wider, within the bound.
A program may use at most 64 MiB of HBM per device.

```python
import jax
import jax.numpy as jnp
from jax import lax

AUX = 1536
VIRT = 1024
TILE = 64
PAIRINGS = 2
OCC_DEV = 1
BLOCKS = 64
ORBS = 64
SLICES = 4
A_TILES = 4
B_TILES = 16
CAP = 56
LOW = 24


def draw_tile_lists(key, part):
    row_count = PAIRINGS * BLOCKS * SLICES
    tile_total = A_TILES * B_TILES
    counts = jax.random.randint(jax.random.fold_in(key, 11), (PAIRINGS, BLOCKS, SLICES), LOW, CAP + 1)
    fullest = jax.random.randint(jax.random.fold_in(key, 12), (PAIRINGS, BLOCKS, 1), 0, SLICES)
    slices = jnp.arange(SLICES, dtype=jnp.int32)[None, None, :]
    counts = jnp.where(slices == fullest, CAP, counts)
    order_keys = jax.random.split(jax.random.fold_in(key, 13), row_count)
    orders = jax.vmap(lambda one_key: jax.random.permutation(one_key, tile_total))(order_keys)
    chosen = orders[:, :CAP].reshape(PAIRINGS, BLOCKS, SLICES, CAP).astype(jnp.int32)
    places = jnp.arange(CAP, dtype=jnp.int32)
    return jnp.where(places < counts[..., None], chosen, -1).astype(jnp.int32)


def steps_of(stream_key, extent, shards, least, top_value):
    level = 1.0
    for dim, blocks in shards:
        heights = jax.random.uniform(jax.random.fold_in(jax.random.fold_in(stream_key, 6), dim), (blocks,), jnp.float32, least / len(shards), top_value / len(shards))
        level = level * jnp.repeat(jnp.exp(heights), extent[dim] // blocks).reshape((-1,) + (1,) * (len(extent) - 1 - dim))
    return level


def centred(key, extent, width, limit, cuts=(), kind=jnp.bfloat16):
    array = jax.random.normal(key, extent, jnp.float32) * width
    if len(cuts) > 0:
        array = steps_of(key, extent, cuts, -0.22, 0.18) * array
    return jnp.clip(array, min=-limit, max=limit).astype(kind)


def setup_inputs(seed: int = 0) -> dict:
    key_list = jax.random.split(jax.random.key(seed), 6)
    integrals = centred(key_list[0], (ORBS, VIRT, AUX), ((AUX + AUX // 4) ** -0.25), 2.0, ((0, 64), (1, 4)))
    occupied_energy = jnp.clip(jax.random.uniform(key_list[1], (ORBS,), jnp.float32, -2.0, -0.2), -2.0, -0.2)
    virtual_energy = jnp.clip(jax.random.uniform(key_list[2], (VIRT,), jnp.float32, 0.5, 4.0), 0.5, 4.0)
    partner_list = jax.vmap(lambda own: jax.random.permutation(own, BLOCKS))(jax.random.split(key_list[3], PAIRINGS)).reshape((PAIRINGS, BLOCKS)).astype(jnp.int32)
    tile_lists = draw_tile_lists(jax.random.fold_in(key_list[5], 71), 0)
    return {"integrals": integrals, "occupied_energy": occupied_energy, "virtual_energy": virtual_energy, "partner_list": partner_list, "tile_lists": tile_lists}


def tiles_of(source):
    orbitals, row_count, aux_width = source.shape
    tile_count = row_count // TILE
    shaped = source.reshape(orbitals, tile_count, TILE, aux_width)
    return shaped.transpose(1, 0, 2, 3).reshape(tile_count, orbitals * TILE, aux_width)


def reference(integrals, occupied_energy, virtual_energy, partner_list, tile_lists):
    orbitals = OCC_DEV
    energy_rows = virtual_energy.reshape(B_TILES, TILE)

    def one_block(block_id):
        start = (block_id * orbitals).astype(jnp.int32)
        own_tiles = tiles_of(lax.dynamic_slice_in_dim(integrals, start, orbitals, 0))
        own_energy = lax.dynamic_slice_in_dim(occupied_energy, start, orbitals, 0)
        totals = jnp.zeros((B_TILES, orbitals * TILE, AUX), jnp.float32)
        for pairing in range(PAIRINGS):
            partner_start = (partner_list[pairing, block_id] * orbitals).astype(jnp.int32)
            partner_tiles = tiles_of(lax.dynamic_slice_in_dim(integrals, partner_start, orbitals, 0))
            partner_energy = lax.dynamic_slice_in_dim(occupied_energy, partner_start, orbitals, 0)
            for slice_id in range(SLICES):
                entries = tile_lists[pairing, block_id, slice_id]
                in_use = entries >= 0
                clamped = jnp.maximum(entries, 0)
                a_tile = (slice_id * A_TILES + clamped // B_TILES).astype(jnp.int32)
                c_tile = (clamped % B_TILES).astype(jnp.int32)
                own_rows = own_tiles[a_tile].astype(jnp.float32)
                partner_rows = partner_tiles[c_tile].astype(jnp.float32)
                scores = jnp.einsum("gxp,gyp->gxy", own_rows, partner_rows)
                gap_left = (energy_rows[a_tile][:, None, :] - own_energy[None, :, None]).reshape(CAP, orbitals * TILE)
                gap_right = (energy_rows[c_tile][:, None, :] - partner_energy[None, :, None]).reshape(CAP, orbitals * TILE)
                ratio = scores / (gap_left[:, :, None] + gap_right[:, None, :])
                amplitude = jnp.where(in_use[:, None, None], ratio, jnp.zeros_like(ratio))
                amplitude = lax.optimization_barrier(amplitude.astype(jnp.bfloat16)).astype(jnp.float32)
                contrib = jnp.einsum("gxy,gyp->gxp", amplitude, partner_rows)
                totals = totals.at[a_tile].add(contrib)
        shaped = totals.reshape(B_TILES, orbitals, TILE, AUX).transpose(1, 0, 2, 3)
        return shaped.reshape(orbitals, VIRT, AUX)

    block_ids = jnp.arange(BLOCKS, dtype=jnp.int32)
    return lax.map(one_block, block_ids).reshape(ORBS, VIRT, AUX)
```

```python
import jax
import jax.numpy as jnp
from jax import lax
from jax.experimental import pallas as pl
from jax.experimental.pallas import tpu as pltpu
from jax.sharding import PartitionSpec as P

MESH = pl.DeviceIdType.MESH
TILE = 64
NY, NZ = 4, 8
BLOCKS = 64
PR, PC = 16, 384


def occ_of(l, y, z):
    return (y * NZ + z) * 2 + l


def z_step(idx):
    odd = lax.rem(idx, 2)
    return odd * lax.div(idx + 1, 2) + (1 - odd) * lax.rem(NZ - lax.div(idx, 2), NZ)


def kernel(
    plist, lists, gap_left, gap_right, own, out,
    recv1, send2, other, final, weights, hits,
    ss1, rs1, ss2, rsa, rso, ssx, rsx, ssc, rsc,
):
    occ = lax.axis_index("occ")
    virt = lax.axis_index("virt")
    l = lax.rem(occ, 2)
    z = lax.rem(lax.div(occ, 2), NZ)
    y = lax.div(occ, 2 * NZ)
    h = lax.div(virt, 2)
    c = lax.rem(virt, 2)
    hv = (1 - h) * 2 + c
    far = (occ, hv)
    near = (occ_of(1 - l, y, z), virt)
    cross = (occ_of(1 - l, y, z), hv)
    sibling = (occ, h * 2 + 1 - c)
    sib_virt = h * 2 + 1 - c
    sib_hv = (1 - h) * 2 + 1 - c

    def remote(src, dst, send, recv, device):
        return pltpu.make_async_remote_copy(
            src_ref=src, dst_ref=dst, send_sem=send, recv_sem=recv, device_id=device, device_id_type=MESH
        )

    barrier = pltpu.get_barrier_semaphore()

    def greet(q, carry):
        tl = lax.rem(l + lax.rem(q, 2), 2)
        ty = lax.rem(y + lax.rem(lax.div(q, 2), NY), NY)
        tz = lax.rem(z + lax.div(q, 2 * NY), NZ)
        pl.semaphore_signal(barrier, inc=1, device_id=(occ_of(tl, ty, tz), virt), device_id_type=MESH)
        return carry

    lax.fori_loop(1, BLOCKS, greet, 0)
    for device in (far, cross, sibling):
        pl.semaphore_signal(barrier, inc=1, device_id=device, device_id_type=MESH)
    pl.semaphore_wait(barrier, BLOCKS - 1 + 3)

    def piece(tl, ty, tz):
        row = pl.multiple_of((2 * tz + tl) * PR, PR)
        col = pl.multiple_of(ty * PC, 128)
        return own.at[pl.ds(row, PR), pl.ds(col, PC)]

    def spread(dz, q):
        tl = lax.rem(l + lax.rem(q, 2), 2)
        ty = lax.rem(y + lax.div(q, 2), NY)
        tz = lax.rem(z + dz, NZ)
        remote(piece(tl, ty, tz), recv1.at[occ], ss1, rs1, (occ_of(tl, ty, tz), virt)).start()

    def spread_group(n, carry):
        dz = z_step(NZ - 1 - n)

        def one(q, inner):
            spread(dz, q)
            return inner

        return lax.fori_loop(0, 2 * NY, one, carry)

    lax.fori_loop(0, NZ - 1, spread_group, 0)

    def spread_here(q, carry):
        spread(0, q)
        return carry

    lax.fori_loop(1, 2 * NY, spread_here, 0)
    pltpu.make_async_copy(piece(l, y, z), recv1.at[occ], rs1).start()

    out[...] = jnp.zeros_like(out)
    row_id = lax.broadcasted_iota(jnp.int32, (16, 256), 0)
    col_id = lax.broadcasted_iota(jnp.int32, (16, 256), 1)
    entry = lax.rem(row_id, 4) * 16 + lax.rem(lax.div(col_id, 32), 4) * 4 + lax.div(row_id, 4)
    first = col_id < 128
    slots = lists.shape[0] // 2

    def look(j, found):
        listed = jnp.where(first, lists[j], lists[slots + j])
        return jnp.where(entry == listed, jnp.float32(1), found)

    hits[...] = lax.fori_loop(0, slots, look, jnp.zeros((16, 256), jnp.float32))

    def weigh(zi, carry):
        right = gap_right[pl.ds(zi, 1), :]
        for a in range(4):
            rows = pl.ds(a * TILE, TILE)
            hit = hits[pl.ds(lax.div(zi, 2) * 4 + a, 1), :]
            weights[zi, rows, :] = hit / (gap_left[rows, :] + right)
        return carry

    lax.fori_loop(0, NZ, weigh, 0)

    pltpu.make_async_copy(recv1, recv1, rs1).wait()

    def pick(idx):
        tz = lax.rem(z + z_step(idx), NZ)

        def one(ty, carry):
            for tl in range(2):
                for k in range(2):
                    partner = plist[k * BLOCKS + occ_of(tl, ty, tz)]
                    send2[tz, ty, tl, k] = recv1[partner]
            return carry

        lax.fori_loop(0, NY, one, 0)

    def deliver(idx, first_y, sem):
        tz = lax.rem(z + z_step(idx), NZ)

        def one(dy, carry):
            ty = lax.rem(y + dy, NY)
            target = (occ_of(l, ty, tz), virt)
            remote(send2.at[tz, ty, l], final.at[:, virt, y, z, l], sem, rsa.at[idx], target).start()
            remote(send2.at[tz, ty, 1 - l], other.at[:, y, z], sem, rso.at[idx], target).start()
            return carry

        lax.fori_loop(first_y, NY, one, 0)

    pick(jnp.int32(0))
    pick(jnp.int32(1))
    pltpu.make_async_copy(send2.at[z, y, l], final.at[:, virt, y, z, l], rsa.at[0]).start()
    pltpu.make_async_copy(send2.at[z, y, 1 - l], other.at[:, y, z], rso.at[0]).start()
    deliver(jnp.int32(0), 1, ss2.at[0])

    def stage2(idx, carry):
        pick(idx + 1)
        deliver(idx, 0, ss2.at[1])
        return carry

    lax.fori_loop(1, NZ - 1, stage2, 0)
    deliver(jnp.int32(NZ - 1), 0, ss2.at[1])

    def await_(ref, sem):
        pltpu.make_async_copy(ref, ref, sem).wait()

    def step(t, carry):
        @pl.when(t < NZ)
        def _():
            zs = lax.rem(z - z_step(t) + NZ, NZ)
            mine = final.at[:, virt, :, zs, l]
            await_(mine, rsa.at[t])
            await_(other.at[:, :, zs], rso.at[t])
            remote(mine, mine, ssx, rsx.at[0, t], far).start()
            remote(other.at[:, :, zs], mine, ssx, rsx.at[1, t], near).start()
            remote(other.at[:, :, zs], mine, ssx, rsx.at[2, t], cross).start()
            remote(mine, mine, ssc, rsc.at[0, t], sibling).start()

        @pl.when((t >= 1) & (t < NZ + 1))
        def _():
            u = t - 1
            zs = lax.rem(z - z_step(u) + NZ, NZ)
            for n, place in enumerate((
                final.at[:, hv, :, zs, l], final.at[:, virt, :, zs, 1 - l], final.at[:, hv, :, zs, 1 - l],
            )):
                await_(place, rsx.at[n, u])
                remote(place, place, ssc, rsc.at[n + 1, u], sibling).start()

        @pl.when(t >= 2)
        def _():
            u = t - 2
            zs = lax.rem(z - z_step(u) + NZ, NZ)
            for n, place in enumerate((
                final.at[:, sib_virt, :, zs, l], final.at[:, sib_hv, :, zs, l],
                final.at[:, sib_virt, :, zs, 1 - l], final.at[:, sib_hv, :, zs, 1 - l],
            )):
                await_(place, rsc.at[n, u])
            rows = jnp.concatenate(
                [final[:, :, yi, zs].reshape(256, PC) for yi in range(NY)], axis=1
            )
            scores = lax.dot_general(
                own[...], rows, (((1,), (1,)), ((), ())), preferred_element_type=jnp.float32
            )
            amplitudes = (scores * weights[zs]).astype(jnp.bfloat16)
            out[...] += jnp.dot(amplitudes, rows, preferred_element_type=jnp.float32)

        return carry

    lax.fori_loop(0, NZ + 2, step, 0)

    await_(recv1.at[pl.ds(0, BLOCKS - 1)], ss1)
    await_(send2.at[0, pl.ds(0, NY - 1)], ss2.at[0])
    await_(send2.at[pl.ds(0, NZ - 1)], ss2.at[1])
    await_(final.at[0, pl.ds(0, 3)], ssx)
    await_(final.at[0], ssc)


def body(integrals, occupied_energy, virtual_energy, partner_list, tile_lists):
    _, rows, aux = integrals.shape
    myself = lax.axis_index("occ")
    slice_id = lax.axis_index("virt")
    slices = lax.axis_size("virt")
    bf16 = jnp.bfloat16
    left = lax.dynamic_slice_in_dim(virtual_energy, slice_id * rows, rows, 0) - occupied_energy[myself]
    right = virtual_energy.reshape(slices, NZ, 2 * PR).transpose(1, 0, 2).reshape(NZ, 1, slices * 2 * PR)
    partner_energy = occupied_energy[partner_list[:, myself]]
    right = (right - partner_energy[None, :, None]).reshape(NZ, 2 * slices * 2 * PR)
    dma = pltpu.SemaphoreType.DMA
    vmem = pl.BlockSpec(memory_space=pltpu.VMEM)
    smem = pl.BlockSpec(memory_space=pltpu.SMEM)
    gradient = pl.pallas_call(
        kernel,
        out_shape=jax.ShapeDtypeStruct((rows, aux), jnp.float32),
        in_specs=[smem, smem, vmem, vmem, vmem],
        out_specs=vmem,
        scratch_shapes=[
            pltpu.VMEM((BLOCKS, PR, PC), bf16),
            pltpu.VMEM((NZ, NY, 2, 2, PR, PC), bf16),
            pltpu.VMEM((2, NY, NZ, PR, PC), bf16),
            pltpu.VMEM((2, slices, NY, NZ, 2, PR, PC), bf16),
            pltpu.VMEM((NZ, rows, 2 * slices * 2 * PR), jnp.float32),
            pltpu.VMEM((16, 256), jnp.float32),
            dma, dma, dma((2,)), dma((NZ,)), dma((NZ,)), dma, dma((3, NZ)), dma, dma((4, NZ)),
        ],
        compiler_params=pltpu.CompilerParams(
            collective_id=0, has_side_effects=True, vmem_limit_bytes=48 * 1024 * 1024
        ),
        name="gradient",
    )(
        partner_list.reshape(-1), tile_lists.reshape(-1), left.reshape(rows, 1), right, integrals.reshape(rows, aux),
    )
    return gradient.reshape(1, rows, aux)


def solution(mesh):
    return jax.shard_map(
        body,
        mesh=mesh,
        in_specs=(P("occ", "virt", None), P(), P(), P(), P(None, "occ", "virt", None)),
        out_specs=P("occ", "virt", None),
        check_vma=False,
    )
```

```python
import jax
import jax.numpy as jnp
from jax import lax
from jax.experimental import pallas as pl
from jax.experimental.pallas import tpu as pltpu
from jax.sharding import PartitionSpec as P

MESH = pl.DeviceIdType.MESH
TILE = 64
NY, NZ = 4, 8
BLOCKS = 64
HALVES = 2
PR, PC = 8, 384
STEPS = HALVES * NZ
SECOND = 2


def occ_of(l, y, z):
    return (y * NZ + z) * 2 + l


def z_step(idx):
    odd = lax.rem(idx, 2)
    return odd * lax.div(idx + 1, 2) + (1 - odd) * lax.rem(NZ - lax.div(idx, 2), NZ)


def kernel(
    plist_in, lists_in, occupied_in, virtual_in, integrals, out,
    plist, lists, occupied, virtual, own, recv_one, recv_two, send_one, send_two,
    other, final, weights, hits, gap_left, gap_right,
    load, ss1, rs1, ss2, rsa, rso, ssx, rsx, ssc, rsc,
):
    occ = lax.axis_index("occ")
    virt = lax.axis_index("virt")
    l = lax.rem(occ, 2)
    z = lax.rem(lax.div(occ, 2), NZ)
    y = lax.div(occ, 2 * NZ)
    h = lax.div(virt, 2)
    c = lax.rem(virt, 2)
    hv = (1 - h) * 2 + c
    far = (occ, hv)
    near = (occ_of(1 - l, y, z), virt)
    cross = (occ_of(1 - l, y, z), hv)
    sibling = (occ, h * 2 + 1 - c)
    sib_virt = h * 2 + 1 - c
    sib_hv = (1 - h) * 2 + 1 - c
    recv = (recv_one, recv_two)
    send = (send_one, send_two)

    def remote(src, dst, send_sem, recv_sem, device):
        return pltpu.make_async_remote_copy(
            src_ref=src, dst_ref=dst, send_sem=send_sem, recv_sem=recv_sem, device_id=device, device_id_type=MESH
        )

    fetches = [
        pltpu.make_async_copy(src, dst, load.at[n])
        for n, (src, dst) in enumerate((
            (integrals.at[0], own), (plist_in, plist), (lists_in, lists),
            (occupied_in, occupied), (virtual_in, virtual),
        ))
    ]
    for fetch in fetches:
        fetch.start()

    barrier = pltpu.get_barrier_semaphore()

    def greet(q, carry):
        tl = lax.rem(l + lax.rem(q, 2), 2)
        ty = lax.rem(y + lax.rem(lax.div(q, 2), NY), NY)
        tz = lax.rem(z + lax.div(q, 2 * NY), NZ)
        pl.semaphore_signal(barrier, inc=1, device_id=(occ_of(tl, ty, tz), virt), device_id_type=MESH)
        return carry

    lax.fori_loop(1, BLOCKS, greet, 0)
    for device in (far, cross, sibling):
        pl.semaphore_signal(barrier, inc=1, device_id=device, device_id_type=MESH)
    for fetch in fetches:
        fetch.wait()
    pl.semaphore_wait(barrier, BLOCKS - 1 + 3)

    def piece(half, tl, ty, tz):
        row = pl.multiple_of(half * 128 + (2 * tz + tl) * PR, PR)
        col = pl.multiple_of(ty * PC, 128)
        return own.at[pl.ds(row, PR), pl.ds(col, PC)]

    for half in range(HALVES):

        def spread(dz, q, half=half):
            tl = lax.rem(l + lax.rem(q, 2), 2)
            ty = lax.rem(y + lax.div(q, 2), NY)
            tz = lax.rem(z + dz, NZ)
            target = (occ_of(tl, ty, tz), virt)
            remote(piece(half, tl, ty, tz), recv[half].at[occ], ss1.at[half], rs1.at[half], target).start()

        def spread_group(n, carry, spread=spread):
            dz = z_step(NZ - 1 - n)

            def one(q, inner):
                spread(dz, q)
                return inner

            return lax.fori_loop(0, 2 * NY, one, carry)

        def spread_here(q, carry, spread=spread):
            spread(0, q)
            return carry

        lax.fori_loop(0, NZ - 1, spread_group, 0)
        lax.fori_loop(1, 2 * NY, spread_here, 0)
        pltpu.make_async_copy(piece(half, l, y, z), recv[half].at[occ], rs1.at[half]).start()

    out[...] = jnp.zeros_like(out)
    row_id = lax.broadcasted_iota(jnp.int32, (16, 128), 0)
    col_id = lax.broadcasted_iota(jnp.int32, (16, 128), 1)
    entry = lax.rem(row_id, 4) * 16 + lax.rem(lax.div(col_id, 16), 4) * 4 + lax.div(row_id, 4)
    first = col_id < 64
    slots = lists.shape[-1]

    def look(j, found):
        listed = jnp.where(first, lists[0, 0, 0, j], lists[1, 0, 0, j])
        return jnp.where(entry == listed, jnp.float32(1), found)

    hits[...] = lax.fori_loop(0, slots, look, jnp.zeros((16, 128), jnp.float32))
    for part in range(2):
        row = virtual[pl.ds(2 * virt + part, 1), :] - occupied[occ]
        gap_left[pl.ds(part * 128, 128), :] = jnp.transpose(jnp.broadcast_to(row, (128, 128)))
    lane = lax.broadcasted_iota(jnp.int32, (1, 128), 1)
    segment = lax.div(lane, 16)
    partner_energy = jnp.where(lane < 64, occupied[plist[0, occ]], occupied[plist[1, occ]])
    for half in range(HALVES):
        for zi in range(NZ):
            right = jnp.zeros((1, 128), jnp.float32)
            for g in range(8):
                row = virtual[2 * (g % 4) + half : 2 * (g % 4) + half + 1, :]
                shift = 16 * (g - zi) % 128
                right = jnp.where(segment == g, pltpu.roll(row, shift, 1) if shift else row, right)
            gap_right[half * NZ + zi : half * NZ + zi + 1, :] = right - partner_energy

    def weigh(n, carry):
        right = gap_right[pl.ds(n, 1), :]
        for a in range(4):
            rows = pl.ds(a * TILE, TILE)
            hit = hits[pl.ds(lax.div(n, 4) * 4 + a, 1), :]
            weights[n, rows, :] = hit / (gap_left[rows, :] + right)
        return carry

    lax.fori_loop(0, STEPS, weigh, 0)

    def stage2(half):
        def pick(idx):
            tz = lax.rem(z + z_step(idx), NZ)

            def one(ty, carry):
                for tl in range(2):
                    for k in range(2):
                        partner = plist[k, occ_of(tl, ty, tz)]
                        send[half][tz, ty, tl, k] = recv[half][partner]
                return carry

            lax.fori_loop(0, NY, one, 0)

        def deliver(idx, first_y, sem):
            tz = lax.rem(z + z_step(idx), NZ)

            def one(dy, carry):
                ty = lax.rem(y + dy, NY)
                target = (occ_of(l, ty, tz), virt)
                place = half * NZ + idx
                remote(
                    send[half].at[tz, ty, l], final.at[half, :, virt, y, z, l], sem, rsa.at[place], target
                ).start()
                remote(send[half].at[tz, ty, 1 - l], other.at[half, :, y, z], sem, rso.at[place], target).start()
                return carry

            lax.fori_loop(first_y, NY, one, 0)

        pltpu.make_async_copy(recv[half], recv[half], rs1.at[half]).wait()
        pick(jnp.int32(0))
        pick(jnp.int32(1))
        mine = rsa.at[half * NZ]
        pltpu.make_async_copy(send[half].at[z, y, l], final.at[half, :, virt, y, z, l], mine).start()
        theirs = rso.at[half * NZ]
        pltpu.make_async_copy(send[half].at[z, y, 1 - l], other.at[half, :, y, z], theirs).start()
        deliver(jnp.int32(0), 1, ss2.at[half, 0])

        def rest(idx, carry):
            pick(idx + 1)
            deliver(idx, 0, ss2.at[half, 1])
            return carry

        lax.fori_loop(1, NZ - 1, rest, 0)
        deliver(jnp.int32(NZ - 1), 0, ss2.at[half, 1])

    def await_(ref, sem):
        pltpu.make_async_copy(ref, ref, sem).wait()

    def source(u):
        return lax.rem(z - z_step(lax.rem(u, NZ)) + NZ, NZ)

    def rows_of(u):
        half = lax.div(u, NZ)
        zs = source(u)
        return jnp.concatenate(
            [final[half, :, :, yi, zs].reshape(128, PC) for yi in range(NY)], axis=1
        )

    def step(t, carry):
        @pl.when(t < STEPS)
        def _():
            half = lax.div(t, NZ)
            zs = source(t)
            mine = final.at[half, :, virt, :, zs, l]
            theirs = other.at[half, :, :, zs]
            await_(mine, rsa.at[t])
            await_(theirs, rso.at[t])
            remote(mine, mine, ssx, rsx.at[0, t], far).start()
            remote(theirs, mine, ssx, rsx.at[1, t], near).start()
            remote(theirs, mine, ssx, rsx.at[2, t], cross).start()
            remote(mine, mine, ssc, rsc.at[0, t], sibling).start()

        @pl.when((t >= 2) & (t < STEPS + 2))
        def _():
            u = t - 2
            half = lax.div(u, NZ)
            zs = source(u)
            for n, place in enumerate((
                final.at[half, :, hv, :, zs, l],
                final.at[half, :, virt, :, zs, 1 - l],
                final.at[half, :, hv, :, zs, 1 - l],
            )):
                await_(place, rsx.at[n, u])
                remote(place, place, ssc, rsc.at[n + 1, u], sibling).start()

        @pl.when((t >= 5) & (lax.rem(t, 2) == 1))
        def _():
            for u in (t - 5, t - 4):
                half = lax.div(u, NZ)
                zs = source(u)
                for n, place in enumerate((
                    final.at[half, :, sib_virt, :, zs, l],
                    final.at[half, :, sib_hv, :, zs, l],
                    final.at[half, :, sib_virt, :, zs, 1 - l],
                    final.at[half, :, sib_hv, :, zs, 1 - l],
                )):
                    await_(place, rsc.at[n, u])
            rows = jnp.concatenate([rows_of(t - 5), rows_of(t - 4)], axis=0)
            scores = lax.dot_general(
                own[...], rows, (((1,), (1,)), ((), ())), preferred_element_type=jnp.float32
            )
            scale = jnp.concatenate(
                [weights[lax.div(u, NZ) * NZ + source(u)] for u in (t - 5, t - 4)], axis=1
            )
            amplitudes = (scores * scale).astype(jnp.bfloat16)
            out[...] += jnp.dot(amplitudes, rows, preferred_element_type=jnp.float32)

        @pl.when(t == SECOND - 1)
        def _():
            stage2(1)

        return carry

    stage2(0)
    lax.fori_loop(0, STEPS + 4, step, 0)

    for half in range(HALVES):
        await_(recv[half].at[pl.ds(0, BLOCKS - 1)], ss1.at[half])
        await_(send[half].at[0, pl.ds(0, NY - 1)], ss2.at[half, 0])
        await_(send[half].at[pl.ds(0, NZ - 1)], ss2.at[half, 1])
    await_(final.at[0, :, pl.ds(0, 3)], ssx)
    await_(final.at[0], ssc)


def body(integrals, occupied_energy, virtual_energy, partner_list, tile_lists):
    _, rows, aux = integrals.shape
    slices = lax.axis_size("virt")
    bf16, f32 = jnp.bfloat16, jnp.float32
    dma = pltpu.SemaphoreType.DMA
    hbm = pl.BlockSpec(memory_space=pltpu.HBM)
    gradient = pl.pallas_call(
        kernel,
        out_shape=jax.ShapeDtypeStruct((rows, aux), f32),
        in_specs=[hbm] * 5,
        out_specs=pl.BlockSpec(memory_space=pltpu.VMEM),
        scratch_shapes=[
            pltpu.SMEM(partner_list.shape, jnp.int32),
            pltpu.SMEM(tile_lists.shape, jnp.int32),
            pltpu.SMEM(occupied_energy.shape, f32),
            pltpu.VMEM((8, 128), f32),
            pltpu.VMEM((rows, aux), bf16),
            pltpu.VMEM((BLOCKS, PR, PC), bf16),
            pltpu.VMEM((BLOCKS, PR, PC), bf16),
            pltpu.VMEM((NZ, NY, 2, 2, PR, PC), bf16),
            pltpu.VMEM((NZ, NY, 2, 2, PR, PC), bf16),
            pltpu.VMEM((HALVES, 2, NY, NZ, PR, PC), bf16),
            pltpu.VMEM((HALVES, 2, slices, NY, NZ, 2, PR, PC), bf16),
            pltpu.VMEM((STEPS, rows, 128), f32),
            pltpu.VMEM((16, 128), f32),
            pltpu.VMEM((rows, 128), f32),
            pltpu.VMEM((STEPS, 128), f32),
            dma((5,)), dma((HALVES,)), dma((HALVES,)), dma((HALVES, 2)), dma((STEPS,)), dma((STEPS,)),
            dma, dma((3, STEPS)), dma, dma((4, STEPS)),
        ],
        compiler_params=pltpu.CompilerParams(
            collective_id=0, has_side_effects=True, vmem_limit_bytes=48 * 1024 * 1024
        ),
        name="gradient",
    )(*[pltpu.with_memory_space_constraint(a, pltpu.HBM) for a in (partner_list, tile_lists, occupied_energy, virtual_energy.reshape(8, 128), integrals)])
    return gradient.reshape(1, rows, aux)


def solution(mesh):
    return jax.shard_map(
        body,
        mesh=mesh,
        in_specs=(P("occ", "virt", None), P(), P(), P(), P(None, "occ", "virt", None)),
        out_specs=P("occ", "virt", None),
        check_vma=False,
    )
```

```python
import jax
import jax.numpy as jnp
from jax import lax
from jax.experimental import pallas as pl
from jax.experimental.pallas import tpu as pltpu
from jax.sharding import PartitionSpec as P

MESH = pl.DeviceIdType.MESH
TILE = 64
NY, NZ = 4, 8
BLOCKS = 64
HALVES = 2
PR, PC = 8, 384
STEPS = HALVES * NZ
SECOND = 2


def occ_of(l, y, z):
    return (y * NZ + z) * 2 + l


def z_step(idx):
    odd = lax.rem(idx, 2)
    return odd * lax.div(idx + 1, 2) + (1 - odd) * lax.rem(NZ - lax.div(idx, 2), NZ)


def kernel(
    plist_in, lists_in, occupied_in, virtual_in, integrals, out,
    plist, lists, occupied, virtual, own, recv_one, recv_two, send_one, send_two,
    other, final, weights, hits, gap_left, gap_right,
    load, ss1, rs1, ss2, rs2, ssx, rsx, ssc, rsc,
):
    occ = lax.axis_index("occ")
    virt = lax.axis_index("virt")
    l = lax.rem(occ, 2)
    z = lax.rem(lax.div(occ, 2), NZ)
    y = lax.div(occ, 2 * NZ)
    h = lax.div(virt, 2)
    c = lax.rem(virt, 2)
    hv = (1 - h) * 2 + c
    far = (occ, hv)
    near = (occ_of(1 - l, y, z), virt)
    cross = (occ_of(1 - l, y, z), hv)
    sibling = (occ, h * 2 + 1 - c)
    recv = (recv_one, recv_two)
    send = (send_one, send_two)

    def remote(src, dst, send_sem, recv_sem, device):
        return pltpu.make_async_remote_copy(
            src_ref=src, dst_ref=dst, send_sem=send_sem, recv_sem=recv_sem, device_id=device, device_id_type=MESH
        )

    fetches = [
        pltpu.make_async_copy(src, dst, load.at[n])
        for n, (src, dst) in enumerate((
            (integrals.at[0], own), (plist_in, plist), (lists_in, lists),
            (occupied_in, occupied), (virtual_in, virtual),
        ))
    ]
    for fetch in fetches:
        fetch.start()

    barrier = pltpu.get_barrier_semaphore()

    def greet(n, carry):
        tz = lax.rem(z + z_step(NZ - 1 - lax.div(n, 2 * NY)), NZ)
        q = 2 * NY - 1 - lax.rem(n, 2 * NY)
        tl = lax.rem(l + lax.rem(q, 2), 2)
        ty = lax.rem(y + lax.div(q, 2), NY)
        pl.semaphore_signal(barrier, inc=1, device_id=(occ_of(tl, ty, tz), virt), device_id_type=MESH)
        return carry

    lax.fori_loop(0, BLOCKS - 1, greet, 0)
    for device in (far, cross, sibling):
        pl.semaphore_signal(barrier, inc=1, device_id=device, device_id_type=MESH)
    for fetch in fetches:
        fetch.wait()
    pl.semaphore_wait(barrier, BLOCKS - 1 + 3)

    def piece(half, tl, ty, tz):
        row = pl.multiple_of(half * 128 + (2 * tz + tl) * PR, PR)
        col = pl.multiple_of(ty * PC, 128)
        return own.at[pl.ds(row, PR), pl.ds(col, PC)]

    for half in range(HALVES):

        def spread(dz, q, half=half):
            tl = lax.rem(l + lax.rem(q, 2), 2)
            ty = lax.rem(y + lax.div(q, 2), NY)
            tz = lax.rem(z + dz, NZ)
            target = (occ_of(tl, ty, tz), virt)
            remote(piece(half, tl, ty, tz), recv[half].at[occ], ss1.at[half], rs1.at[half], target).start()

        def spread_group(n, carry, spread=spread):
            dz = z_step(NZ - 1 - n)

            def one(q, inner):
                spread(dz, q)
                return inner

            return lax.fori_loop(0, 2 * NY, one, carry)

        def spread_here(q, carry, spread=spread):
            spread(0, q)
            return carry

        lax.fori_loop(0, NZ - 1, spread_group, 0)
        lax.fori_loop(1, 2 * NY, spread_here, 0)
        pltpu.make_async_copy(piece(half, l, y, z), recv[half].at[occ], rs1.at[half]).start()

    out[...] = jnp.zeros_like(out)
    row_id = lax.broadcasted_iota(jnp.int32, (16, 128), 0)
    col_id = lax.broadcasted_iota(jnp.int32, (16, 128), 1)
    entry = lax.rem(row_id, 4) * 16 + lax.rem(lax.div(col_id, 16), 4) * 4 + lax.div(row_id, 4)
    first = col_id < 64
    slots = lists.shape[-1]

    def look(j, found):
        listed = jnp.where(first, lists[0, 0, 0, j], lists[1, 0, 0, j])
        return jnp.where(entry == listed, jnp.float32(1), found)

    hits[...] = lax.fori_loop(0, slots, look, jnp.zeros((16, 128), jnp.float32))
    for part in range(2):
        row = virtual[pl.ds(2 * virt + part, 1), :] - occupied[occ]
        gap_left[pl.ds(part * 128, 128), :] = jnp.transpose(jnp.broadcast_to(row, (128, 128)))
    lane = lax.broadcasted_iota(jnp.int32, (1, 128), 1)
    segment = lax.div(lane, 16)
    partner_energy = jnp.where(lane < 64, occupied[plist[0, occ]], occupied[plist[1, occ]])
    for half in range(HALVES):
        for zi in range(NZ):
            right = jnp.zeros((1, 128), jnp.float32)
            for g in range(8):
                row = virtual[2 * (g % 4) + half : 2 * (g % 4) + half + 1, :]
                shift = 16 * (g - zi) % 128
                right = jnp.where(segment == g, pltpu.roll(row, shift, 1) if shift else row, right)
            gap_right[half * NZ + zi : half * NZ + zi + 1, :] = right - partner_energy

    def weigh(n, carry):
        right = gap_right[pl.ds(n, 1), :]
        for a in range(4):
            rows = pl.ds(a * TILE, TILE)
            hit = hits[pl.ds(lax.div(n, 4) * 4 + a, 1), :]
            weights[n, rows, :] = hit / (gap_left[rows, :] + right)
        return carry

    lax.fori_loop(0, STEPS, weigh, 0)

    def stage2(half):
        def pick(idx):
            tz = lax.rem(z + z_step(idx), NZ)

            def one(ty, carry):
                for tl in range(2):
                    for k in range(2):
                        partner = plist[k, occ_of(tl, ty, tz)]
                        send[half][tz, ty, tl, k] = recv[half][partner]
                return carry

            lax.fori_loop(0, NY, one, 0)

        def deliver(idx, first_y, sem):
            tz = lax.rem(z + z_step(idx), NZ)

            def one(dy, carry):
                ty = lax.rem(y + dy, NY)
                target = (occ_of(l, ty, tz), virt)
                place = half * NZ + idx
                remote(
                    send[half].at[tz, ty, l], final.at[half, :, virt, y, z, l], sem, rs2.at[place], target
                ).start()
                remote(send[half].at[tz, ty, 1 - l], other.at[half, :, y, z], sem, rs2.at[place], target).start()
                return carry

            lax.fori_loop(first_y, NY, one, 0)

        pltpu.make_async_copy(recv[half], recv[half], rs1.at[half]).wait()
        pick(jnp.int32(0))
        pick(jnp.int32(1))
        here = rs2.at[half * NZ]
        pltpu.make_async_copy(send[half].at[z, y, l], final.at[half, :, virt, y, z, l], here).start()
        pltpu.make_async_copy(send[half].at[z, y, 1 - l], other.at[half, :, y, z], here).start()
        deliver(jnp.int32(0), 1, ss2.at[half, 0])

        def rest(idx, carry):
            pick(idx + 1)
            deliver(idx, 0, ss2.at[half, 1])
            return carry

        lax.fori_loop(1, NZ - 1, rest, 0)
        deliver(jnp.int32(NZ - 1), 0, ss2.at[half, 1])

    def await_(ref, sem):
        pltpu.make_async_copy(ref, ref, sem).wait()

    def source(u):
        return lax.rem(z - z_step(lax.rem(u, NZ)) + NZ, NZ)

    def rows_of(u):
        half = lax.div(u, NZ)
        zs = source(u)
        return jnp.concatenate(
            [final[half, :, :, yi, zs].reshape(128, PC) for yi in range(NY)], axis=1
        )

    def step(t, carry):
        @pl.when(t < STEPS)
        def _():
            half = lax.div(t, NZ)
            zs = source(t)
            mine = final.at[half, :, virt, :, zs, l]
            theirs = other.at[half, :, :, zs]
            await_(final.at[half, 0, 0, 0], rs2.at[t])
            remote(mine, mine, ssx, rsx.at[t], far).start()
            remote(theirs, mine, ssx, rsx.at[t], near).start()
            remote(theirs, mine, ssx, rsx.at[t], cross).start()
            remote(mine, mine, ssc, rsc.at[lax.div(t, 2)], sibling).start()

        @pl.when((t >= 3) & (t < STEPS + 3))
        def _():
            u = t - 3
            half = lax.div(u, NZ)
            zs = source(u)
            await_(final.at[half, 0, 0, pl.ds(0, 3), pl.ds(0, 4)], rsx.at[u])
            for place in (
                final.at[half, :, hv, :, zs, l],
                final.at[half, :, virt, :, zs, 1 - l],
                final.at[half, :, hv, :, zs, 1 - l],
            ):
                remote(place, place, ssc, rsc.at[lax.div(u, 2)], sibling).start()

        @pl.when((t >= 6) & (lax.rem(t, 2) == 0))
        def _():
            await_(final.at[0, 0, 0], rsc.at[lax.div(t - 6, 2)])
            rows = jnp.concatenate([rows_of(t - 6), rows_of(t - 5)], axis=0)
            scores = lax.dot_general(
                own[...], rows, (((1,), (1,)), ((), ())), preferred_element_type=jnp.float32
            )
            scale = jnp.concatenate(
                [weights[lax.div(u, NZ) * NZ + source(u)] for u in (t - 6, t - 5)], axis=1
            )
            amplitudes = (scores * scale).astype(jnp.bfloat16)
            out[...] += jnp.dot(amplitudes, rows, preferred_element_type=jnp.float32)

        @pl.when(t == SECOND - 1)
        def _():
            stage2(1)

        return carry

    stage2(0)
    lax.fori_loop(0, STEPS + 5, step, 0)

    for half in range(HALVES):
        await_(recv[half].at[pl.ds(0, BLOCKS - 1)], ss1.at[half])
        await_(send[half].at[0, pl.ds(0, NY - 1)], ss2.at[half, 0])
        await_(send[half].at[pl.ds(0, NZ - 1)], ss2.at[half, 1])
    await_(final.at[0, :, pl.ds(0, 3)], ssx)
    await_(final.at[0], ssc)


def body(integrals, occupied_energy, virtual_energy, partner_list, tile_lists):
    _, rows, aux = integrals.shape
    slices = lax.axis_size("virt")
    bf16, f32 = jnp.bfloat16, jnp.float32
    dma = pltpu.SemaphoreType.DMA
    hbm = pl.BlockSpec(memory_space=pltpu.HBM)
    gradient = pl.pallas_call(
        kernel,
        out_shape=jax.ShapeDtypeStruct((rows, aux), f32),
        in_specs=[hbm] * 5,
        out_specs=pl.BlockSpec(memory_space=pltpu.VMEM),
        scratch_shapes=[
            pltpu.SMEM(partner_list.shape, jnp.int32),
            pltpu.SMEM(tile_lists.shape, jnp.int32),
            pltpu.SMEM(occupied_energy.shape, f32),
            pltpu.VMEM((8, 128), f32),
            pltpu.VMEM((rows, aux), bf16),
            pltpu.VMEM((BLOCKS, PR, PC), bf16),
            pltpu.VMEM((BLOCKS, PR, PC), bf16),
            pltpu.VMEM((NZ, NY, 2, 2, PR, PC), bf16),
            pltpu.VMEM((NZ, NY, 2, 2, PR, PC), bf16),
            pltpu.VMEM((HALVES, 2, NY, NZ, PR, PC), bf16),
            pltpu.VMEM((HALVES, 2, slices, NY, NZ, 2, PR, PC), bf16),
            pltpu.VMEM((STEPS, rows, 128), f32),
            pltpu.VMEM((16, 128), f32),
            pltpu.VMEM((rows, 128), f32),
            pltpu.VMEM((STEPS, 128), f32),
            dma((5,)), dma((HALVES,)), dma((HALVES,)), dma((HALVES, 2)), dma((STEPS,)),
            dma, dma((STEPS,)), dma, dma((STEPS // 2,)),
        ],
        compiler_params=pltpu.CompilerParams(
            collective_id=0, has_side_effects=True, vmem_limit_bytes=48 * 1024 * 1024
        ),
        name="gradient",
    )(*[pltpu.with_memory_space_constraint(a, pltpu.HBM) for a in (partner_list, tile_lists, occupied_energy, virtual_energy.reshape(8, 128), integrals)])
    return gradient.reshape(1, rows, aux)


def solution(mesh):
    return jax.shard_map(
        body,
        mesh=mesh,
        in_specs=(P("occ", "virt", None), P(), P(), P(), P(None, "occ", "virt", None)),
        out_specs=P("occ", "virt", None),
        check_vma=False,
    )
```

```python
import jax
import jax.numpy as jnp
from jax import lax
from jax.experimental import pallas as pl
from jax.experimental.pallas import tpu as pltpu
from jax.sharding import PartitionSpec as P

MESH = pl.DeviceIdType.MESH
TILE = 64
NY, NZ = 4, 8
BLOCKS = 64
HALVES = 2
PR, PC = 8, 384
STEPS = HALVES * NZ
SECOND = 2


def occ_of(l, y, z):
    return (y * NZ + z) * 2 + l


def z_step(idx):
    odd = lax.rem(idx, 2)
    return odd * lax.div(idx + 1, 2) + (1 - odd) * lax.rem(NZ - lax.div(idx, 2), NZ)


def kernel(
    plist_in, lists_in, occupied_in, virtual_in, integrals, out,
    plist, lists, occupied, virtual, own, recv_one, recv_two, send_one, send_two,
    other, final, weights, hits, gap_left, gap_right,
    load, ss1, rs1, ss2, rs2, ssx, rsx, ssc, rsc,
):
    occ = lax.axis_index("occ")
    virt = lax.axis_index("virt")
    l = lax.rem(occ, 2)
    z = lax.rem(lax.div(occ, 2), NZ)
    y = lax.div(occ, 2 * NZ)
    h = lax.div(virt, 2)
    c = lax.rem(virt, 2)
    hv = (1 - h) * 2 + c
    far = (occ, hv)
    near = (occ_of(1 - l, y, z), virt)
    cross = (occ_of(1 - l, y, z), hv)
    sibling = (occ, h * 2 + 1 - c)
    recv = (recv_one, recv_two)
    send = (send_one, send_two)

    def remote(src, dst, send_sem, recv_sem, device):
        return pltpu.make_async_remote_copy(
            src_ref=src, dst_ref=dst, send_sem=send_sem, recv_sem=recv_sem, device_id=device, device_id_type=MESH
        )

    fetches = [
        pltpu.make_async_copy(src, dst, load.at[n])
        for n, (src, dst) in enumerate((
            (integrals.at[0], own), (plist_in, plist), (lists_in, lists),
            (occupied_in, occupied), (virtual_in, virtual),
        ))
    ]
    for fetch in fetches:
        fetch.start()

    barrier = pltpu.get_barrier_semaphore()

    plane = [
        (lax.rem(l + q % 2, 2), lax.rem(y + q // 2, NY)) for q in range(2 * NY)
    ]
    starts = [occ_of(tl, ty, 0) for tl, ty in plane]

    def greet(occ_id):
        pl.semaphore_signal(barrier, inc=1, device_id=(occ_id, virt), device_id_type=MESH)

    def greet_plane(n, carry):
        tz = lax.rem(z + z_step(NZ - 1 - n), NZ)
        for q in reversed(range(2 * NY)):
            greet(starts[q] + 2 * tz)
        return carry

    lax.fori_loop(0, NZ - 1, greet_plane, 0)
    for q in reversed(range(1, 2 * NY)):
        greet(starts[q] + 2 * z)
    for device in (far, cross, sibling):
        pl.semaphore_signal(barrier, inc=1, device_id=device, device_id_type=MESH)
    for fetch in fetches:
        fetch.wait()
    pl.semaphore_wait(barrier, BLOCKS - 1 + 3)

    def piece(half, tl, ty, tz):
        row = pl.multiple_of(half * 128 + (2 * tz + tl) * PR, PR)
        col = pl.multiple_of(ty * PC, 128)
        return own.at[pl.ds(row, PR), pl.ds(col, PC)]

    for half in range(HALVES):

        def spread(q, tz, half=half):
            tl, ty = plane[q]
            target = (starts[q] + 2 * tz, virt)
            remote(piece(half, tl, ty, tz), recv[half].at[occ], ss1.at[half], rs1.at[half], target).start()

        def spread_plane(n, carry, spread=spread):
            tz = lax.rem(z + z_step(NZ - 1 - n), NZ)
            for q in range(2 * NY):
                spread(q, tz)
            return carry

        lax.fori_loop(0, NZ - 1, spread_plane, 0)
        for q in range(1, 2 * NY):
            spread(q, z)
        pltpu.make_async_copy(piece(half, l, y, z), recv[half].at[occ], rs1.at[half]).start()

    out[...] = jnp.zeros_like(out)
    row_id = lax.broadcasted_iota(jnp.int32, (16, 128), 0)
    col_id = lax.broadcasted_iota(jnp.int32, (16, 128), 1)
    entry = lax.rem(row_id, 4) * 16 + lax.rem(lax.div(col_id, 16), 4) * 4 + lax.div(row_id, 4)
    first = col_id < 64
    slots = lists.shape[-1]

    def look(j, found):
        listed = jnp.where(first, lists[0, 0, 0, j], lists[1, 0, 0, j])
        return jnp.where(entry == listed, jnp.float32(1), found)

    hits[...] = lax.fori_loop(0, slots, look, jnp.zeros((16, 128), jnp.float32))
    for part in range(2):
        row = virtual[pl.ds(2 * virt + part, 1), :] - occupied[occ]
        gap_left[pl.ds(part * 128, 128), :] = jnp.transpose(jnp.broadcast_to(row, (128, 128)))
    lane = lax.broadcasted_iota(jnp.int32, (1, 128), 1)
    segment = lax.div(lane, 16)
    partner_energy = jnp.where(lane < 64, occupied[plist[0, occ]], occupied[plist[1, occ]])
    for half in range(HALVES):
        for zi in range(NZ):
            right = jnp.zeros((1, 128), jnp.float32)
            for g in range(8):
                row = virtual[2 * (g % 4) + half : 2 * (g % 4) + half + 1, :]
                shift = 16 * (g - zi) % 128
                right = jnp.where(segment == g, pltpu.roll(row, shift, 1) if shift else row, right)
            gap_right[half * NZ + zi : half * NZ + zi + 1, :] = right - partner_energy

    def weigh(n, carry):
        right = gap_right[pl.ds(n, 1), :]
        for a in range(4):
            rows = pl.ds(a * TILE, TILE)
            hit = hits[pl.ds(lax.div(n, 4) * 4 + a, 1), :]
            weights[n, rows, :] = hit / (gap_left[rows, :] + right)
        return carry

    lax.fori_loop(0, STEPS, weigh, 0)

    def stage2(half):
        def pick(idx):
            tz = lax.rem(z + z_step(idx), NZ)

            def one(ty, carry):
                for tl in range(2):
                    for k in range(2):
                        partner = plist[k, occ_of(tl, ty, tz)]
                        send[half][tz, ty, tl, k] = recv[half][partner]
                return carry

            lax.fori_loop(0, NY, one, 0)

        def deliver(idx, first_y, sem):
            tz = lax.rem(z + z_step(idx), NZ)

            def one(dy, carry):
                ty = lax.rem(y + dy, NY)
                target = (occ_of(l, ty, tz), virt)
                place = half * NZ + idx
                remote(
                    send[half].at[tz, ty, l], final.at[half, :, virt, y, z, l], sem, rs2.at[place], target
                ).start()
                remote(send[half].at[tz, ty, 1 - l], other.at[half, :, y, z], sem, rs2.at[place], target).start()
                return carry

            lax.fori_loop(first_y, NY, one, 0)

        pltpu.make_async_copy(recv[half], recv[half], rs1.at[half]).wait()
        pick(jnp.int32(0))
        pick(jnp.int32(1))
        here = rs2.at[half * NZ]
        pltpu.make_async_copy(send[half].at[z, y, l], final.at[half, :, virt, y, z, l], here).start()
        pltpu.make_async_copy(send[half].at[z, y, 1 - l], other.at[half, :, y, z], here).start()
        deliver(jnp.int32(0), 1, ss2.at[half, 0])

        def rest(idx, carry):
            pick(idx + 1)
            deliver(idx, 0, ss2.at[half, 1])
            return carry

        lax.fori_loop(1, NZ - 1, rest, 0)
        deliver(jnp.int32(NZ - 1), 0, ss2.at[half, 1])

    def await_(ref, sem):
        pltpu.make_async_copy(ref, ref, sem).wait()

    def source(u):
        return lax.rem(z - z_step(lax.rem(u, NZ)) + NZ, NZ)

    def rows_of(u):
        half = lax.div(u, NZ)
        zs = source(u)
        return jnp.concatenate(
            [final[half, :, :, yi, zs].reshape(128, PC) for yi in range(NY)], axis=1
        )

    def step(t, carry):
        @pl.when(t < STEPS)
        def _():
            half = lax.div(t, NZ)
            zs = source(t)
            mine = final.at[half, :, virt, :, zs, l]
            theirs = other.at[half, :, :, zs]
            await_(final.at[half, 0, 0, 0], rs2.at[t])
            remote(mine, mine, ssx, rsx.at[t], far).start()
            remote(theirs, mine, ssx, rsx.at[t], near).start()
            remote(theirs, mine, ssx, rsx.at[t], cross).start()
            remote(mine, mine, ssc, rsc.at[lax.div(t, 2)], sibling).start()

        @pl.when((t >= 3) & (t < STEPS + 3))
        def _():
            u = t - 3
            half = lax.div(u, NZ)
            zs = source(u)
            await_(final.at[half, 0, 0, pl.ds(0, 3), pl.ds(0, 4)], rsx.at[u])
            for place in (
                final.at[half, :, hv, :, zs, l],
                final.at[half, :, virt, :, zs, 1 - l],
                final.at[half, :, hv, :, zs, 1 - l],
            ):
                remote(place, place, ssc, rsc.at[lax.div(u, 2)], sibling).start()

        @pl.when((t >= 6) & (lax.rem(t, 2) == 0))
        def _():
            await_(final.at[0, 0, 0], rsc.at[lax.div(t - 6, 2)])
            rows = jnp.concatenate([rows_of(t - 6), rows_of(t - 5)], axis=0)
            scores = lax.dot_general(
                own[...], rows, (((1,), (1,)), ((), ())), preferred_element_type=jnp.float32
            )
            scale = jnp.concatenate(
                [weights[lax.div(u, NZ) * NZ + source(u)] for u in (t - 6, t - 5)], axis=1
            )
            amplitudes = (scores * scale).astype(jnp.bfloat16)
            out[...] += jnp.dot(amplitudes, rows, preferred_element_type=jnp.float32)

        @pl.when(t == SECOND - 1)
        def _():
            stage2(1)

        return carry

    stage2(0)
    lax.fori_loop(0, STEPS + 5, step, 0)

    for half in range(HALVES):
        await_(recv[half].at[pl.ds(0, BLOCKS - 1)], ss1.at[half])
        await_(send[half].at[0, pl.ds(0, NY - 1)], ss2.at[half, 0])
        await_(send[half].at[pl.ds(0, NZ - 1)], ss2.at[half, 1])
    await_(final.at[0, :, pl.ds(0, 3)], ssx)
    await_(final.at[0], ssc)


def body(integrals, occupied_energy, virtual_energy, partner_list, tile_lists):
    _, rows, aux = integrals.shape
    slices = lax.axis_size("virt")
    bf16, f32 = jnp.bfloat16, jnp.float32
    dma = pltpu.SemaphoreType.DMA
    hbm = pl.BlockSpec(memory_space=pltpu.HBM)
    gradient = pl.pallas_call(
        kernel,
        out_shape=jax.ShapeDtypeStruct((rows, aux), f32),
        in_specs=[hbm] * 5,
        out_specs=pl.BlockSpec(memory_space=pltpu.VMEM),
        scratch_shapes=[
            pltpu.SMEM(partner_list.shape, jnp.int32),
            pltpu.SMEM(tile_lists.shape, jnp.int32),
            pltpu.SMEM(occupied_energy.shape, f32),
            pltpu.VMEM((8, 128), f32),
            pltpu.VMEM((rows, aux), bf16),
            pltpu.VMEM((BLOCKS, PR, PC), bf16),
            pltpu.VMEM((BLOCKS, PR, PC), bf16),
            pltpu.VMEM((NZ, NY, 2, 2, PR, PC), bf16),
            pltpu.VMEM((NZ, NY, 2, 2, PR, PC), bf16),
            pltpu.VMEM((HALVES, 2, NY, NZ, PR, PC), bf16),
            pltpu.VMEM((HALVES, 2, slices, NY, NZ, 2, PR, PC), bf16),
            pltpu.VMEM((STEPS, rows, 128), f32),
            pltpu.VMEM((16, 128), f32),
            pltpu.VMEM((rows, 128), f32),
            pltpu.VMEM((STEPS, 128), f32),
            dma((5,)), dma((HALVES,)), dma((HALVES,)), dma((HALVES, 2)), dma((STEPS,)),
            dma, dma((STEPS,)), dma, dma((STEPS // 2,)),
        ],
        compiler_params=pltpu.CompilerParams(
            collective_id=0, has_side_effects=True, vmem_limit_bytes=48 * 1024 * 1024
        ),
        name="gradient",
    )(*[pltpu.with_memory_space_constraint(a, pltpu.HBM) for a in (partner_list, tile_lists, occupied_energy, virtual_energy.reshape(8, 128), integrals)])
    return gradient.reshape(1, rows, aux)


def solution(mesh):
    return jax.shard_map(
        body,
        mesh=mesh,
        in_specs=(P("occ", "virt", None), P(), P(), P(), P(None, "occ", "virt", None)),
        out_specs=P("occ", "virt", None),
        check_vma=False,
    )
```

```python
import jax
import jax.numpy as jnp
from jax import lax
from jax.experimental import pallas as pl
from jax.experimental.pallas import tpu as pltpu
from jax.sharding import PartitionSpec as P

MESH = pl.DeviceIdType.MESH
TILE = 64
NY, NZ = 4, 8
BLOCKS = 64
HALVES = 2
PR, PC = 8, 384
STEPS = HALVES * NZ
SECOND = 2


def occ_of(l, y, z):
    return (y * NZ + z) * 2 + l


def z_step(idx):
    odd = lax.rem(idx, 2)
    return odd * lax.div(idx + 1, 2) + (1 - odd) * lax.rem(NZ - lax.div(idx, 2), NZ)


def kernel(
    plist_in, lists_in, occupied_in, virtual_in, integrals, out,
    plist, lists, occupied, virtual, own, recv_one, recv_two, send_one, send_two,
    other, final, weights, hits, gap_left, gap_right,
    load, ss1, rs1, ss2, rs2, ssx, rsx, ssc, rsc,
):
    occ = lax.axis_index("occ")
    virt = lax.axis_index("virt")
    l = lax.rem(occ, 2)
    z = lax.rem(lax.div(occ, 2), NZ)
    y = lax.div(occ, 2 * NZ)
    h = lax.div(virt, 2)
    c = lax.rem(virt, 2)
    hv = (1 - h) * 2 + c
    far = (occ, hv)
    near = (occ_of(1 - l, y, z), virt)
    cross = (occ_of(1 - l, y, z), hv)
    sibling = (occ, h * 2 + 1 - c)
    recv = (recv_one, recv_two)
    send = (send_one, send_two)

    def remote(src, dst, send_sem, recv_sem, device):
        return pltpu.make_async_remote_copy(
            src_ref=src, dst_ref=dst, send_sem=send_sem, recv_sem=recv_sem, device_id=device, device_id_type=MESH
        )

    fetches = [
        pltpu.make_async_copy(src, dst, load.at[n])
        for n, (src, dst) in enumerate((
            (integrals.at[0], own), (plist_in, plist), (lists_in, lists),
            (occupied_in, occupied), (virtual_in, virtual),
        ))
    ]
    for fetch in fetches:
        fetch.start()

    barrier = pltpu.get_barrier_semaphore()

    plane = [
        (lax.rem(l + q % 2, 2), lax.rem(y + q // 2, NY)) for q in range(2 * NY)
    ]
    starts = [occ_of(tl, ty, 0) for tl, ty in plane]

    def greet(occ_id):
        pl.semaphore_signal(barrier, inc=1, device_id=(occ_id, virt), device_id_type=MESH)

    def greet_plane(n, carry):
        tz = lax.rem(z + z_step(NZ - 1 - n), NZ)
        for q in reversed(range(2 * NY)):
            greet(starts[q] + 2 * tz)
        return carry

    lax.fori_loop(0, NZ - 1, greet_plane, 0)
    for q in reversed(range(1, 2 * NY)):
        greet(starts[q] + 2 * z)
    for device in (far, cross, sibling):
        pl.semaphore_signal(barrier, inc=1, device_id=device, device_id_type=MESH)
    for fetch in fetches:
        fetch.wait()
    pl.semaphore_wait(barrier, BLOCKS - 1 + 3)

    def piece(half, tl, ty, tz):
        row = pl.multiple_of(half * 128 + (2 * tz + tl) * PR, PR)
        col = pl.multiple_of(ty * PC, 128)
        return own.at[pl.ds(row, PR), pl.ds(col, PC)]

    for half in range(HALVES):

        def spread(q, tz, half=half):
            tl, ty = plane[q]
            target = (starts[q] + 2 * tz, virt)
            remote(piece(half, tl, ty, tz), recv[half].at[occ], ss1.at[half], rs1.at[half], target).start()

        def spread_plane(n, carry, spread=spread):
            tz = lax.rem(z + z_step(NZ - 1 - n), NZ)
            for q in range(2 * NY):
                spread(q, tz)
            return carry

        lax.fori_loop(0, NZ - 1, spread_plane, 0)
        for q in range(1, 2 * NY):
            spread(q, z)
        pltpu.make_async_copy(piece(half, l, y, z), recv[half].at[occ], rs1.at[half]).start()

    out[...] = jnp.zeros_like(out)
    row_id = lax.broadcasted_iota(jnp.int32, (16, 128), 0)
    col_id = lax.broadcasted_iota(jnp.int32, (16, 128), 1)
    entry = lax.rem(row_id, 4) * 16 + lax.rem(lax.div(col_id, 16), 4) * 4 + lax.div(row_id, 4)
    first = col_id < 64
    slots = lists.shape[-1]

    def look(j, found):
        listed = jnp.where(first, lists[0, 0, 0, j], lists[1, 0, 0, j])
        return jnp.where(entry == listed, jnp.float32(1), found)

    hits[...] = lax.fori_loop(0, slots, look, jnp.zeros((16, 128), jnp.float32))
    for part in range(2):
        row = virtual[pl.ds(2 * virt + part, 1), :] - occupied[occ]
        gap_left[pl.ds(part * 128, 128), :] = jnp.transpose(jnp.broadcast_to(row, (128, 128)))
    lane = lax.broadcasted_iota(jnp.int32, (1, 128), 1)
    segment = lax.div(lane, 16)
    partner_energy = jnp.where(lane < 64, occupied[plist[0, occ]], occupied[plist[1, occ]])
    for half in range(HALVES):
        for zi in range(NZ):
            right = jnp.zeros((1, 128), jnp.float32)
            for g in range(8):
                row = virtual[2 * (g % 4) + half : 2 * (g % 4) + half + 1, :]
                shift = 16 * (g - zi) % 128
                right = jnp.where(segment == g, pltpu.roll(row, shift, 1) if shift else row, right)
            gap_right[half * NZ + zi : half * NZ + zi + 1, :] = right - partner_energy

    def weigh(n, carry):
        right = gap_right[pl.ds(n, 1), :]
        for a in range(4):
            rows = pl.ds(a * TILE, TILE)
            hit = hits[pl.ds(lax.div(n, 4) * 4 + a, 1), :]
            weights[n, rows, :] = hit / (gap_left[rows, :] + right)
        return carry

    lax.fori_loop(0, STEPS, weigh, 0)

    def stage2(half):
        def pick(idx):
            tz = lax.rem(z + z_step(idx), NZ)

            for ty in range(NY):
                for tl in range(2):
                    for k in range(2):
                        partner = plist[k, occ_of(tl, ty, 0) + 2 * tz]
                        send[half][tz, ty, tl, k] = recv[half][partner]

        def deliver(idx, first_y, sem):
            tz = lax.rem(z + z_step(idx), NZ)

            place = half * NZ + idx
            for dy in range(first_y, NY):
                ty = plane[2 * dy][1]
                target = (starts[2 * dy] + 2 * tz, virt)
                arrival = rs2.at[place]
                remote(send[half].at[tz, ty, l], final.at[half, :, virt, y, z, l], sem, arrival, target).start()
                remote(send[half].at[tz, ty, 1 - l], other.at[half, :, y, z], sem, arrival, target).start()

        pltpu.make_async_copy(recv[half], recv[half], rs1.at[half]).wait()
        pick(jnp.int32(0))
        pick(jnp.int32(1))
        here = rs2.at[half * NZ]
        pltpu.make_async_copy(send[half].at[z, y, l], final.at[half, :, virt, y, z, l], here).start()
        pltpu.make_async_copy(send[half].at[z, y, 1 - l], other.at[half, :, y, z], here).start()
        deliver(jnp.int32(0), 1, ss2.at[half, 0])

        def rest(idx, carry):
            pick(idx + 1)
            deliver(idx, 0, ss2.at[half, 1])
            return carry

        lax.fori_loop(1, NZ - 1, rest, 0)
        deliver(jnp.int32(NZ - 1), 0, ss2.at[half, 1])

    def await_(ref, sem):
        pltpu.make_async_copy(ref, ref, sem).wait()

    def source(u):
        return lax.rem(z - z_step(lax.rem(u, NZ)) + NZ, NZ)

    def rows_of(u):
        half = lax.div(u, NZ)
        zs = source(u)
        return jnp.concatenate(
            [final[half, :, :, yi, zs].reshape(128, PC) for yi in range(NY)], axis=1
        )

    def step(t, carry):
        @pl.when(t < STEPS)
        def _():
            half = lax.div(t, NZ)
            zs = source(t)
            mine = final.at[half, :, virt, :, zs, l]
            theirs = other.at[half, :, :, zs]
            await_(final.at[half, 0, 0, 0], rs2.at[t])
            remote(mine, mine, ssx, rsx.at[t], far).start()
            remote(theirs, mine, ssx, rsx.at[t], near).start()
            remote(theirs, mine, ssx, rsx.at[t], cross).start()
            remote(mine, mine, ssc, rsc.at[lax.div(t, 2)], sibling).start()

        @pl.when((t >= 3) & (t < STEPS + 3))
        def _():
            u = t - 3
            half = lax.div(u, NZ)
            zs = source(u)
            await_(final.at[half, 0, 0, pl.ds(0, 3), pl.ds(0, 4)], rsx.at[u])
            for place in (
                final.at[half, :, hv, :, zs, l],
                final.at[half, :, virt, :, zs, 1 - l],
                final.at[half, :, hv, :, zs, 1 - l],
            ):
                remote(place, place, ssc, rsc.at[lax.div(u, 2)], sibling).start()

        @pl.when((t >= 6) & (lax.rem(t, 2) == 0))
        def _():
            await_(final.at[0, 0, 0], rsc.at[lax.div(t - 6, 2)])
            rows = jnp.concatenate([rows_of(t - 6), rows_of(t - 5)], axis=0)
            scores = lax.dot_general(
                own[...], rows, (((1,), (1,)), ((), ())), preferred_element_type=jnp.float32
            )
            scale = jnp.concatenate(
                [weights[lax.div(u, NZ) * NZ + source(u)] for u in (t - 6, t - 5)], axis=1
            )
            amplitudes = (scores * scale).astype(jnp.bfloat16)
            out[...] += jnp.dot(amplitudes, rows, preferred_element_type=jnp.float32)

        @pl.when(t == SECOND - 1)
        def _():
            stage2(1)

        return carry

    stage2(0)
    lax.fori_loop(0, STEPS + 5, step, 0)

    for half in range(HALVES):
        await_(recv[half].at[pl.ds(0, BLOCKS - 1)], ss1.at[half])
        await_(send[half].at[0, pl.ds(0, NY - 1)], ss2.at[half, 0])
        await_(send[half].at[pl.ds(0, NZ - 1)], ss2.at[half, 1])
    await_(final.at[0, :, pl.ds(0, 3)], ssx)
    await_(final.at[0], ssc)


def body(integrals, occupied_energy, virtual_energy, partner_list, tile_lists):
    _, rows, aux = integrals.shape
    slices = lax.axis_size("virt")
    bf16, f32 = jnp.bfloat16, jnp.float32
    dma = pltpu.SemaphoreType.DMA
    hbm = pl.BlockSpec(memory_space=pltpu.HBM)
    gradient = pl.pallas_call(
        kernel,
        out_shape=jax.ShapeDtypeStruct((rows, aux), f32),
        in_specs=[hbm] * 5,
        out_specs=pl.BlockSpec(memory_space=pltpu.VMEM),
        scratch_shapes=[
            pltpu.SMEM(partner_list.shape, jnp.int32),
            pltpu.SMEM(tile_lists.shape, jnp.int32),
            pltpu.SMEM(occupied_energy.shape, f32),
            pltpu.VMEM((8, 128), f32),
            pltpu.VMEM((rows, aux), bf16),
            pltpu.VMEM((BLOCKS, PR, PC), bf16),
            pltpu.VMEM((BLOCKS, PR, PC), bf16),
            pltpu.VMEM((NZ, NY, 2, 2, PR, PC), bf16),
            pltpu.VMEM((NZ, NY, 2, 2, PR, PC), bf16),
            pltpu.VMEM((HALVES, 2, NY, NZ, PR, PC), bf16),
            pltpu.VMEM((HALVES, 2, slices, NY, NZ, 2, PR, PC), bf16),
            pltpu.VMEM((STEPS, rows, 128), f32),
            pltpu.VMEM((16, 128), f32),
            pltpu.VMEM((rows, 128), f32),
            pltpu.VMEM((STEPS, 128), f32),
            dma((5,)), dma((HALVES,)), dma((HALVES,)), dma((HALVES, 2)), dma((STEPS,)),
            dma, dma((STEPS,)), dma, dma((STEPS // 2,)),
        ],
        compiler_params=pltpu.CompilerParams(
            collective_id=0, has_side_effects=True, vmem_limit_bytes=48 * 1024 * 1024
        ),
        name="gradient",
    )(*[pltpu.with_memory_space_constraint(a, pltpu.HBM) for a in (partner_list, tile_lists, occupied_energy, virtual_energy.reshape(8, 128), integrals)])
    return gradient.reshape(1, rows, aux)


def solution(mesh):
    return jax.shard_map(
        body,
        mesh=mesh,
        in_specs=(P("occ", "virt", None), P(), P(), P(), P(None, "occ", "virt", None)),
        out_specs=P("occ", "virt", None),
        check_vma=False,
    )
```
